32 devices in a mesh: gx: 8 (over z, core), gy: 4 (over y, x).
Axes of the slice: x: 2, y: 2, z: 4, core: 2. Of those that a mesh axis runs over, the one named last changes fastest.
Arguments:
- p_prev: float32 [48, 1024, 512], P(None, 'gx', 'gy'), may hold values from -6 to 6
- p_cur: float32 [48, 1024, 512], P(None, 'gx', 'gy'), may hold values from -6 to 6
- courant: float32 [48, 1024, 512], P(None, 'gx', 'gy'), may hold values from 0.04 to 0.2
- snapshots: bfloat16 [3, 48, 1024, 512], P(None, None, 'gx', 'gy'), may hold values from -6 to 6
- residual: float32 [4, 65536, 128], P(None, ('gx', 'gy')), may hold values from -6 to 6
- rec_owner: int32 [65536, 1], P(('gx', 'gy')), may hold values from 0 to 31; in each aligned block of 2048 rows (0 to 2047, 2048 to 4095, ...) at most 128 rows name the same one
- rec_cell: int32 [65536], P(('gx', 'gy')), may hold values from 0 to 16383
- signs: int32 [4], replicated, may hold values from -1 to 1, as said below
Outputs:
- adjoint_field: float32 [48, 1024, 512], P(None, 'gx', 'gy')
- image: float32 [48, 1024, 512], P(None, 'gx', 'gy')
The draws below stay inside these ranges and needn't reach their ends.
Inputs may be any that keep to these rules, and one draw needn't show every extreme that they name: `rec_owner`: in the rows of one device no owner is named more than 128 times, a bound that some block reaches. `signs`: each entry is +1 or -1, and both occur.
All inputs are finite; a program needn't handle non-finite values.
Results may differ from the reference program's by a relative error of at most 0.0003.
Values sent between devices are 32-bit elements; how exact they have to be, the bound alone decides.
A program may use at most 128 MiB of HBM per device.

```python
import math
import jax
import jax.numpy as jnp
import numpy as np
from jax import lax

NZ = 48
CX = 128
CY = 128
STEPS = 3
SHOTS = 4
NT = 128
RECV_DEPTH = 2
RECV_DEV = 2048
CAP = 128
NX = 1024
NY = 512
RECV = 65536
N_GY = 4
DEVICES = 32


def draw_signs(key, part):
    order = jax.random.permutation(key, jnp.arange(SHOTS))
    return (2 * (order % 2) - 1).astype(jnp.int32)


def plant(result, stream_key, low, high):
    dims = result.shape
    place = [jax.random.randint(jax.random.fold_in(stream_key, axis), (), 0, dims[axis]) for axis in range(len(dims))]
    result = result.at[tuple(place)].set(low)
    longest = dims.index(max(dims))
    place[longest] = (place[longest] + 1) % dims[longest]
    return result.at[tuple(place)].set(high)


def steps_of(key, extent, pieces, smallest, top_value):
    level = 1.0
    for position, blocks in pieces:
        heights = jax.random.uniform(jax.random.fold_in(jax.random.fold_in(key, 6), position), (blocks,), jnp.float32, smallest / len(pieces), top_value / len(pieces))
        level = level * jnp.repeat(jnp.exp(heights), extent[position] // blocks).reshape((-1,) + (1,) * (len(extent) - 1 - position))
    return level


def deal_out(key, own, number, rows, count, top, most, slope):
    order = jax.random.permutation(key, count)
    heavy_load, usual = load_shares(count, rows * top, most, slope, True), load_shares(count, rows * top, most, slope, False)
    places = jnp.arange(count)

    def named(sizes, offset_by):
        used = int((sizes > 0).sum())
        fixed = max(1, used // 4)
        passed = fixed + (places - fixed + offset_by * (used - fixed)) % max(1, count - fixed)
        return jnp.zeros((count,), jnp.int32).at[order[jnp.where(places < fixed, places, passed)]].set(jnp.asarray(sizes, jnp.int32))

    sizes = jnp.where(number % 4 == 0, named(heavy_load, number // 4), named(usual, number - number // 4 - 1))
    mixed = jax.random.permutation(jax.random.fold_in(own, 3), count)
    giver, receiver = mixed[0:count // 2 * 2:2], mixed[1:count // 2 * 2:2]
    room = jnp.minimum(sizes[giver] - 1, most - sizes[receiver]) // 2
    room = jnp.where((giver == order[0]) | (receiver == order[0]) | (sizes[receiver] == 0), 0, jnp.maximum(room, 0))
    passed = jax.random.randint(jax.random.fold_in(own, 4), (count // 2,), 0, 1 << 20) % (room + 1)
    sizes = sizes.at[giver].add(-passed).at[receiver].add(passed)
    labels = jnp.searchsorted(jnp.cumsum(sizes), jnp.arange(rows * top), side="right").astype(jnp.int32)
    listing = labels.reshape(top, rows).T
    listing = listing[jax.random.permutation(jax.random.fold_in(own, 1), rows)]
    offset_by = jax.random.randint(jax.random.fold_in(own, 2), (rows, 1), 0, top)
    return jnp.take_along_axis(listing, (jnp.arange(top)[None, :] + offset_by) % top, axis=1)


def load_shares(number_of, total, bound, skew, full):
    portions = [(1 << 20) // math.isqrt(rank ** skew) + 1 for rank in range(1, number_of + 1)]
    largest = bound if full else min(bound, max(-(-total // number_of), total * portions[0] // sum(portions)))
    least = 1 if total - largest >= number_of - 1 else 0
    holding, surplus = [largest] + [least] * (number_of - 1), total - largest - least * (number_of - 1)
    while surplus > 0:
        movable = [i for i in range(1, number_of) if holding[i] < largest] or [i for i in range(1, number_of) if holding[i] < bound]
        mass, left = sum([portions[i] for i in movable]), surplus
        for i in movable:
            more = min(bound - holding[i], max(1, left * portions[i] // mass), surplus)
            holding[i] = holding[i] + more
            surplus = surplus - more
    return np.array(holding)


def scatter_about(key, extent, scale, limit, shards=(), dtype=jnp.bfloat16):
    values = jax.random.normal(key, extent, jnp.float32) * scale
    if len(shards) > 0:
        values = steps_of(key, extent, shards, -0.22, 0.18) * values
    return jnp.clip(values, min=-limit, max=limit).astype(dtype)


def setup_inputs(seed: int = 0) -> dict:
    key_of = jax.random.split(jax.random.key(seed), 9)
    p_prev = scatter_about(key_of[0], (NZ, NX, NY), 1.0, 6.0, ((1, 8), (2, 4)), jnp.float32)
    p_cur = scatter_about(key_of[1], (NZ, NX, NY), 1.0, 6.0, ((1, 8), (2, 4)), jnp.float32)
    courant = jnp.clip(jnp.exp(math.log(0.2) - 1.609438 * jax.random.uniform(key_of[2], (NZ, NX, NY), jnp.float32) ** steps_of(key_of[2], (NZ, NX, NY), ((1, 8), (2, 4)), -0.2, 0.2)), 0.04, 0.2)
    snapshots = scatter_about(key_of[3], (STEPS, NZ, NX, NY), 1.0, 6.0, ((2, 8), (3, 4)))
    residual = scatter_about(key_of[4], (SHOTS, RECV, NT), 1.0, 6.0, ((1, 32),), jnp.float32)
    rec_owner_keys = jax.random.split(jax.random.fold_in(key_of[5], 1), RECV // RECV_DEV)
    rec_owner_turns = jax.random.permutation(jax.random.fold_in(key_of[5], 3), RECV // RECV_DEV)
    rec_owner = jax.vmap(lambda own, number: deal_out(jax.random.fold_in(key_of[5], 2), own, number, RECV_DEV, DEVICES, 1, CAP, 2))(rec_owner_keys, rec_owner_turns).reshape((RECV, 1))
    rec_cell = plant(jax.random.randint(key_of[6], (RECV,), 0, CX * CY), jax.random.fold_in(key_of[6], 1), 0, (CX * CY) - 1).astype(jnp.int32)
    signs = draw_signs(jax.random.fold_in(key_of[8], 71), 0)
    return {"p_prev": p_prev, "p_cur": p_cur, "courant": courant, "snapshots": snapshots, "residual": residual, "rec_owner": rec_owner, "rec_cell": rec_cell, "signs": signs}


COEFF = (-205.0 / 72.0, 8.0 / 5.0, -1.0 / 5.0, 8.0 / 315.0, -1.0 / 560.0)

def laplace(ext):
    depth = ext.shape[0]
    width_a = ext.shape[1] - 8
    width_b = ext.shape[2] - 8
    center = ext[:, 4:4 + width_a, 4:4 + width_b]
    zpad = jnp.pad(center, ((4, 4), (0, 0), (0, 0)))
    total = 3.0 * COEFF[0] * center
    for i in range(1, 5):
        near = ext[:, 4 + i:4 + i + width_a, 4:4 + width_b] + ext[:, 4 - i:4 - i + width_a, 4:4 + width_b]
        near = near + ext[:, 4:4 + width_a, 4 + i:4 + i + width_b] + ext[:, 4:4 + width_a, 4 - i:4 - i + width_b]
        near = near + zpad[4 + i:4 + i + depth] + zpad[4 - i:4 - i + depth]
        total = total + COEFF[i] * near
    return total

def step_table(samples, steps):
    rows = jnp.arange(samples).astype(jnp.float32)[:, None]
    cols = jnp.arange(steps).astype(jnp.float32)[None, :]
    return jnp.cos(math.pi * (cols + 0.5) * (rows + 0.5) / samples) * math.sqrt(2.0 / samples)

def reference(p_prev, p_cur, courant, snapshots, residual, rec_owner, rec_cell, signs):
    encoded = lax.optimization_barrier(jnp.sum(signs.astype(jnp.float32)[:, None, None] * residual, axis=0))
    amps = jnp.dot(encoded, step_table(NT, STEPS), precision=lax.Precision.HIGHEST)
    owner = rec_owner[:, 0]
    inline = owner // N_GY * CX + rec_cell // CY
    cross = owner % N_GY * CY + rec_cell % CY
    injection = jnp.zeros((STEPS, NX, NY), jnp.float32).at[:, inline, cross].add(amps.T)
    prev, cur = (p_prev, p_cur)
    image = jnp.zeros(p_cur.shape, jnp.float32)
    for k in range(STEPS):
        ext = jnp.pad(cur, ((0, 0), (4, 4), (4, 4)))
        nxt = 2.0 * cur - prev + courant * laplace(ext)
        nxt = nxt.at[RECV_DEPTH].add(courant[RECV_DEPTH] * injection[k])
        image = image + snapshots[k].astype(jnp.float32) * nxt
        prev, cur = (cur, nxt)
    return (cur, image)
```

```python
import functools
import math

import jax
import jax.numpy as jnp
import numpy as np
from jax import lax
from jax.experimental import pallas as pl
from jax.experimental.pallas import tpu as pltpu
from jax.sharding import PartitionSpec as P

STEPS = 3
NT = 128
RECV_DEPTH = 2
HALO = 4
CHUNK = 16
BLOCK = 256

SCALE = 5040.0
CENTER = -205.0 / 72.0 * SCALE
TAPS = (8064.0, -1008.0, 128.0, -9.0)

F32 = jnp.float32
BF16 = jnp.bfloat16
I32 = jnp.int32
MESH = pl.DeviceIdType.MESH


def taps(distance):
    out = jnp.zeros(distance.shape, F32)
    for i, c in enumerate(TAPS):
        out = jnp.where(distance == i + 1, c, out)
    return out


def split(v, axis):
    hi = v.astype(BF16)
    lo = (v - hi.astype(F32)).astype(BF16)
    return jnp.concatenate([hi, lo], axis=axis)


def iota(shape, dim):
    return lax.broadcasted_iota(I32, shape, dim)


def lanes_dot(a, b, **kw):
    return lax.dot_general(a, b, (((1,), (1,)), ((), ())), preferred_element_type=F32, **kw)


def kernel(
    n_gx, n_gy, signs, owner, cell, table, p_prev, p_cur, courant_h, snaps_h, residual_h,
    field_out, image_out,
    buf_a, buf_b, courant, snaps, residual, image, sx, rx, sy, ry, corner, edge, planes,
    snd, got, load_sem, out_sem, sxs, rxs, sys_, rys, snds, gots,
):
    n = n_gx * n_gy
    nz, nx, ny = p_cur.shape
    half, mid = nx // 2, ny // 2
    chunks = nz // CHUNK
    gx, gy = lax.axis_index("gx"), lax.axis_index("gy")
    me = gx * n_gy + gy

    inner = pl.ds(HALO, nz)
    loads = [
        pltpu.make_async_copy(p_cur, buf_a.at[inner], load_sem.at[0]),
        pltpu.make_async_copy(residual_h, residual, load_sem.at[1]),
        pltpu.make_async_copy(p_prev, buf_b.at[inner], load_sem.at[2]),
        pltpu.make_async_copy(courant_h, courant, load_sem.at[3]),
    ] + [pltpu.make_async_copy(snaps_h.at[k], snaps.at[k], load_sem.at[4 + k]) for k in range(STEPS)]
    for load in loads:
        load.start()

    barrier = pltpu.get_barrier_semaphore()

    def greet(o, carry):
        d = lax.rem(me + o, n)
        pl.semaphore_signal(
            barrier, inc=1, device_id=(d // n_gy, lax.rem(d, n_gy)), device_id_type=MESH
        )
        return carry

    lax.fori_loop(1, n, greet, 0)

    band = taps(jnp.abs(iota((nx, nx), 0) - iota((nx, nx), 1))).astype(BF16)
    t_x = jnp.concatenate([band, band], axis=1)
    t_y = jnp.concatenate([band, band], axis=0) if nx == ny else None
    row = iota((16, 16), 0)
    src = iota((16, 16), 1) & 7
    place = jnp.where(src < 4, src - 4, nx + src - 4)
    target = jnp.where(row < 8, row, nx - 16 + row)
    h_x = taps(jnp.abs(place - target)).astype(BF16)
    a, b = iota((ny, ny), 0), iota((ny, ny), 1)
    pos = jnp.where(a < mid, (a & 3) - 4, ny + (a & 3))
    edge_taps = taps(jnp.abs(b - pos))
    group = (a & (mid - 1)) >> 2

    def fill(q, carry):
        c = jnp.where(group == q, edge_taps, 0.0).astype(BF16)
        corner[q, pl.ds(0, ny), :] = c
        corner[q, pl.ds(ny, ny), :] = c
        return carry

    lax.fori_loop(0, CHUNK, fill, 0)
    zero = jnp.zeros((HALO, nx, ny), F32)
    for buf in (buf_a, buf_b):
        buf[pl.ds(0, HALO)] = zero
        buf[pl.ds(HALO + nz, HALO)] = zero

    for side, absent in ((0, gx == 0), (1, gx == n_gx - 1)):

        @pl.when(absent)
        def _(side=side):
            for k in range(STEPS):
                rx[k, side] = jnp.zeros(rx.shape[2:], F32)

    for side, absent in ((0, gy == 0), (1, gy == n_gy - 1)):

        @pl.when(absent)
        def _(side=side):
            for k in range(STEPS):
                ry[k, side] = jnp.zeros(ry.shape[2:], F32)

    lane = iota((half, ny), 1)

    def pack(v, k, g, q):
        z = g * CHUNK + q
        sx[k, 0, z] = v[nx - HALO :]
        sx[k, 1, z] = v[:HALO]
        top, low = v[:half], v[half:]
        first = (lane >> 2) == q
        second = (lane >> 2) == q + mid // 4
        s = 4 * q
        right = sy[k, 0, g]
        right = jnp.where(first, pltpu.roll(top, s + 4, 1), right)
        right = jnp.where(second, pltpu.roll(low, s + mid + 4, 1), right)
        sy[k, 0, g] = right
        left = sy[k, 1, g]
        left = jnp.where(second, pltpu.roll(top, s + mid, 1), left)
        left = jnp.where(first, pltpu.roll(low, s, 1), left)
        sy[k, 1, g] = left

    def halo_copies(k, g):
        zs = pl.ds(g * CHUNK, CHUNK)
        out = []
        for side, step, send_ok, recv_ok in (
            (0, 1, gx < n_gx - 1, gx > 0),
            (1, -1, gx > 0, gx < n_gx - 1),
        ):
            i = (k * chunks + g) * 2 + side
            copy = pltpu.make_async_remote_copy(
                src_ref=sx.at[k, side, zs], dst_ref=rx.at[k, side, zs],
                send_sem=sxs.at[i], recv_sem=rxs.at[i],
                device_id=(lax.rem(gx + step + n_gx, n_gx), gy), device_id_type=MESH,
            )
            out.append((copy, send_ok, recv_ok))
        for side, step, send_ok, recv_ok in (
            (0, 1, gy < n_gy - 1, gy > 0),
            (1, -1, gy > 0, gy < n_gy - 1),
        ):
            i = (k * chunks + g) * 2 + side
            copy = pltpu.make_async_remote_copy(
                src_ref=sy.at[k, side, g], dst_ref=ry.at[k, side, g],
                send_sem=sys_.at[i], recv_sem=rys.at[i],
                device_id=(gx, lax.rem(gy + step + n_gy, n_gy)), device_id_type=MESH,
            )
            out.append((copy, send_ok, recv_ok))
        return out

    def send_halo(k, g):
        for copy, send_ok, _ in halo_copies(k, g):
            pl.when(send_ok)(copy.start)

    def wait_halo(k, g):
        for copy, _, recv_ok in halo_copies(k, g):
            pl.when(recv_ok)(copy.wait_recv)

    order = tuple(range(1, chunks)) + (0,)

    loads[0].wait()
    for g in order:

        def first_pack(q, carry, g=g):
            pack(buf_a[HALO + g * CHUNK + q], 0, g, q)
            return carry

        lax.fori_loop(0, CHUNK, first_pack, 0)
    pl.semaphore_wait(barrier, n - 1)
    for g in order:
        send_halo(0, g)

    loads[1].wait()
    recv_dev = owner.shape[1]
    slots = snd.shape[2]
    upper = (iota((BLOCK, BLOCK), 0) < iota((BLOCK, BLOCK), 1)).astype(F32).astype(BF16)
    count = jnp.zeros((n, 1), F32)
    message = jnp.zeros((n * 8, slots), F32)
    part = iota((8, BLOCK), 0)
    shift = ny.bit_length() - 1
    for blk in range(recv_dev // BLOCK):
        rows = pl.ds(blk * BLOCK, BLOCK)
        enc = signs[0].astype(F32) * residual[0, rows, :]
        for s in range(1, residual.shape[0]):
            enc = enc + signs[s].astype(F32) * residual[s, rows, :]
        amps = lanes_dot(table[...], enc, precision=lax.Precision.HIGHEST)
        hi = amps.astype(BF16).astype(F32)
        c = cell[:, rows]
        at_x = (c >> shift).astype(F32)
        at_y = (c & (ny - 1)).astype(F32)
        payload = jnp.where((part & 1) == 0, hi, amps - hi)
        payload = jnp.where(part == 6, at_x, payload)
        payload = jnp.where(part == 7, at_y, payload)
        onehot = jnp.where(iota((n, BLOCK), 0) == owner[:, rows], 1.0, 0.0)
        before = jnp.dot(onehot.astype(BF16), upper, preferred_element_type=F32) + count
        count = count + jnp.sum(onehot, axis=1, keepdims=True)
        rank = jnp.sum(before * onehot, axis=0, keepdims=True)
        spread = (onehot[:, None, :] * payload[None]).reshape(n * 8, BLOCK).astype(BF16)
        slot = jnp.where(iota((slots, BLOCK), 0).astype(F32) == rank, 1.0, 0.0).astype(BF16)
        message = message + lanes_dot(spread, slot)
    snd[...] = message.reshape(n, 8, slots)
    got[me] = snd[me]

    def message_to(o):
        d = lax.rem(me + o, n)
        return pltpu.make_async_remote_copy(
            src_ref=snd.at[d], dst_ref=got.at[me], send_sem=snds.at[o], recv_sem=gots.at[o],
            device_id=(d // n_gy, lax.rem(d, n_gy)), device_id_type=MESH,
        )

    def post(o, carry):
        message_to(o).start()
        return carry

    lax.fori_loop(1, n, post, 0)

    def step_chunk(k, g, cur, prev):
        wait_halo(k, g)
        left, right = ry[k, 0, g], ry[k, 1, g]
        near = lane < mid
        edges = jnp.concatenate(
            [jnp.where(near, left, right), pltpu.roll(jnp.where(near, right, left), mid, 1)], axis=0
        )
        edge[...] = split(edges, 1)

        def plane(q):
            z = g * CHUNK + q
            v = cur[z + HALO]
            lap = jnp.dot(split(v, 1), t_y, preferred_element_type=F32)
            lap = lap + jnp.dot(edge[...], corner[q], preferred_element_type=F32)
            lap = lap + jnp.dot(t_x, split(v, 0), preferred_element_type=F32)
            over = jnp.concatenate([rx[k, 0, z], rx[k, 1, z]], axis=0)
            over_hi = over.astype(BF16).astype(F32)
            over = jnp.concatenate([over_hi, over - over_hi], axis=0).astype(BF16)
            border = jnp.dot(h_x, over, preferred_element_type=F32)
            depth = (3.0 * CENTER) * v
            for i in range(1, HALO + 1):
                depth = depth + TAPS[i - 1] * (cur[z + HALO + i] + cur[z + HALO - i])
            lap = lap + depth
            lap = jnp.concatenate(
                [lap[:8] + border[:8], lap[8 : nx - 8], lap[nx - 8 :] + border[8:]], axis=0
            )
            nxt = (2.0 * v - prev[z + HALO]) + (courant[z] * (1.0 / SCALE)) * lap
            prev[z + HALO] = nxt
            shot = snaps[k, z].astype(F32) * nxt
            image[z] = shot if k == 0 else image[z] + shot
            if k < STEPS - 1:
                pack(nxt, k + 1, g, q)

        def body(j, carry):
            plane(2 * j)
            plane(2 * j + 1)
            return carry

        lax.fori_loop(0, CHUNK // 2, body, 0)
        if k < STEPS - 1:
            send_halo(k + 1, g)

    def scatter():
        def arrive(o, carry):
            d = lax.rem(me - o + n, n)
            pltpu.make_async_remote_copy(
                src_ref=snd.at[d], dst_ref=got.at[d], send_sem=snds.at[o], recv_sem=gots.at[o],
                device_id=(d // n_gy, lax.rem(d, n_gy)), device_id_type=MESH,
            ).wait_recv()
            return carry

        lax.fori_loop(1, n, arrive, 0)
        planes[...] = jnp.zeros(planes.shape, F32)
        row_x = iota((nx, slots), 0).astype(F32)
        row_y = iota((ny, slots), 0).astype(F32)

        def gather(j, carry):
            lhs = [[] for _ in range(STEPS)]
            rhs = []
            for i in range(4):
                block = got[4 * j + i]
                at_x = row_x == block[6:7]
                at_y = jnp.where(row_y == block[7:8], 1.0, 0.0).astype(BF16)
                for k in range(STEPS):
                    for h in range(2):
                        lhs[k].append(
                            jnp.where(at_x, block[2 * k + h : 2 * k + h + 1], 0.0).astype(BF16)
                        )
                rhs += [at_y, at_y]
            lhs = jnp.concatenate([jnp.concatenate(l, axis=1) for l in lhs], axis=0)
            planes[...] += lanes_dot(lhs, jnp.concatenate(rhs, axis=1))
            return carry

        lax.fori_loop(0, n // 4, gather, 0)

    outs = []
    for load in loads[2:]:
        load.wait()
    for k in range(STEPS):
        cur, prev = (buf_a, buf_b) if k % 2 == 0 else (buf_b, buf_a)
        for g in order:
            if g == RECV_DEPTH // CHUNK:
                if k == 0:
                    scatter()
                at = HALO + RECV_DEPTH
                prev[at] = prev[at] - courant[RECV_DEPTH] * planes[pl.ds(k * nx, nx), :]
            step_chunk(k, g, cur, prev)
            if k == STEPS - 1:
                zs = pl.ds(g * CHUNK, CHUNK)
                outs += [
                    pltpu.make_async_copy(
                        prev.at[pl.ds(HALO + g * CHUNK, CHUNK)], field_out.at[zs], out_sem.at[2 * g]
                    ),
                    pltpu.make_async_copy(image.at[zs], image_out.at[zs], out_sem.at[2 * g + 1]),
                ]
                outs[-2].start()
                outs[-1].start()

    def finish(o, carry):
        message_to(o).wait_send()
        return carry

    lax.fori_loop(1, n, finish, 0)
    for k in range(STEPS):
        for g in order:
            for copy, send_ok, _ in halo_copies(k, g):
                pl.when(send_ok)(copy.wait_send)
    for out in outs:
        out.wait()


def step_table(samples, steps):
    rows = np.arange(samples, dtype=np.float64)[None, :]
    cols = np.repeat(np.arange(steps, dtype=np.float64), 2)[:, None]
    table = np.cos(math.pi * (cols + 0.5) * (rows + 0.5) / samples) * math.sqrt(2.0 / samples)
    return np.concatenate([table, np.zeros((8 - 2 * steps, samples))]).astype(np.float32)


def shards(n_gx, n_gy, p_prev, p_cur, courant, snapshots, residual, rec_owner, rec_cell, signs):
    nz, nx, ny = p_cur.shape
    n = n_gx * n_gy
    recv_dev = rec_cell.shape[0]
    slots = -(-(2 * recv_dev // n) // 128) * 128
    chunks = nz // CHUNK
    anywhere = pl.BlockSpec(memory_space=pl.ANY)
    vmem = pl.BlockSpec(memory_space=pltpu.VMEM)
    dma = pltpu.SemaphoreType.DMA
    whole = jax.ShapeDtypeStruct(p_cur.shape, F32)
    return pl.pallas_call(
        functools.partial(kernel, n_gx, n_gy),
        out_shape=(whole, whole),
        in_specs=[pl.BlockSpec(memory_space=pltpu.SMEM)] + [vmem] * 3 + [anywhere] * 5,
        out_specs=(anywhere, anywhere),
        scratch_shapes=[
            pltpu.VMEM((nz + 2 * HALO, nx, ny), F32),
            pltpu.VMEM((nz + 2 * HALO, nx, ny), F32),
            pltpu.VMEM((nz, nx, ny), F32),
            pltpu.VMEM((STEPS, nz, nx, ny), BF16),
            pltpu.VMEM(residual.shape, F32),
            pltpu.VMEM((nz, nx, ny), F32),
            pltpu.VMEM((STEPS, 2, nz, HALO, ny), F32),
            pltpu.VMEM((STEPS, 2, nz, HALO, ny), F32),
            pltpu.VMEM((STEPS, 2, chunks, nx // 2, ny), F32),
            pltpu.VMEM((STEPS, 2, chunks, nx // 2, ny), F32),
            pltpu.VMEM((CHUNK, 2 * ny, ny), BF16),
            pltpu.VMEM((nx, 2 * ny), BF16),
            pltpu.VMEM((STEPS * nx, ny), F32),
            pltpu.VMEM((n, 8, slots), F32),
            pltpu.VMEM((n, 8, slots), F32),
            dma((4 + STEPS,)),
            dma((2 * chunks,)),
            dma((2 * STEPS * chunks,)),
            dma((2 * STEPS * chunks,)),
            dma((2 * STEPS * chunks,)),
            dma((2 * STEPS * chunks,)),
            dma((n,)),
            dma((n,)),
        ],
        compiler_params=pltpu.CompilerParams(
            collective_id=0, has_side_effects=True, vmem_limit_bytes=60 * 1024 * 1024
        ),
        name="adjoint_steps",
    )(
        signs,
        rec_owner.reshape(1, recv_dev),
        rec_cell.reshape(1, recv_dev),
        jnp.asarray(step_table(NT, STEPS)),
        p_prev, p_cur, courant, snapshots, residual,
    )


def solution(mesh):
    placed = (
        P(None, "gx", "gy"),
        P(None, "gx", "gy"),
        P(None, "gx", "gy"),
        P(None, None, "gx", "gy"),
        P(None, ("gx", "gy"), None),
        P(("gx", "gy"), None),
        P(("gx", "gy")),
        P(),
    )
    return jax.shard_map(
        functools.partial(shards, mesh.shape["gx"], mesh.shape["gy"]),
        mesh=mesh,
        in_specs=placed,
        out_specs=(P(None, "gx", "gy"), P(None, "gx", "gy")),
        check_vma=False,
    )
```

```python
import functools
import math

import jax
import jax.numpy as jnp
import numpy as np
from jax import lax
from jax.experimental import pallas as pl
from jax.experimental.pallas import tpu as pltpu
from jax.sharding import PartitionSpec as P

STEPS = 3
NT = 128
RECV_DEPTH = 2
HALO = 4
CHUNK = 16
BLOCK = 256
GROUP = 4

SCALE = 5040.0
CENTER_Y, CENTER_X = -43008.0, -42.0
TAPS = (8064.0, -1008.0, 128.0, -9.0)

F32 = jnp.float32
BF16 = jnp.bfloat16
I32 = jnp.int32
MESH = pl.DeviceIdType.MESH


def taps(distance):
    out = jnp.zeros(distance.shape, F32)
    for i, c in enumerate(TAPS):
        out = jnp.where(distance == i + 1, c, out)
    return out


def split(v, axis):
    hi = v.astype(BF16)
    lo = (v - hi.astype(F32)).astype(BF16)
    return jnp.concatenate([hi, lo], axis=axis)


def iota(shape, dim):
    return lax.broadcasted_iota(I32, shape, dim)


def lanes_dot(a, b, **kw):
    return lax.dot_general(a, b, (((1,), (1,)), ((), ())), preferred_element_type=F32, **kw)


def kernel(
    n_gx, n_gy, signs, owner, cell, table, p_prev, p_cur, courant_h, snaps_h, residual_h,
    field_out, image_out,
    buf_a, buf_b, courant, snaps, residual, image, sx, rx, sy, ry, edge, planes,
    snd, got, load_sem, out_sem, sxs, rxs, sys_, rys, snds, gots,
):
    n = n_gx * n_gy
    nz, nx, ny = p_cur.shape
    half, mid = nx // 2, ny // 2
    chunks = nz // CHUNK
    gx, gy = lax.axis_index("gx"), lax.axis_index("gy")
    me = gx * n_gy + gy

    inner = pl.ds(HALO, nz)
    loads = [
        pltpu.make_async_copy(p_cur, buf_a.at[inner], load_sem.at[0]),
        pltpu.make_async_copy(residual_h, residual, load_sem.at[1]),
        pltpu.make_async_copy(p_prev, buf_b.at[inner], load_sem.at[2]),
        pltpu.make_async_copy(courant_h, courant, load_sem.at[3]),
    ] + [pltpu.make_async_copy(snaps_h.at[k], snaps.at[k], load_sem.at[4 + k]) for k in range(STEPS)]
    for load in loads:
        load.start()

    barrier = pltpu.get_barrier_semaphore()

    def greet(o, carry):
        d = lax.rem(me + o, n)
        pl.semaphore_signal(
            barrier, inc=1, device_id=(d // n_gy, lax.rem(d, n_gy)), device_id_type=MESH
        )
        return carry

    lax.fori_loop(1, n, greet, 0)

    def band(size, center):
        distance = jnp.abs(iota((size, size), 0) - iota((size, size), 1))
        return jnp.where(distance == 0, center, taps(distance)).astype(BF16)

    t_x = jnp.concatenate([band(nx, CENTER_X)] * 2, axis=1)
    t_y = jnp.concatenate([band(ny, CENTER_Y)] * 2, axis=0)
    row = iota((16, 16), 0)
    src = iota((16, 16), 1) & 7
    place = jnp.where(src < 4, src - 4, nx + src - 4)
    target = jnp.where(row < 8, row, nx - 16 + row)
    h_x = taps(jnp.abs(place - target)).astype(BF16)
    a, b = iota((ny, ny), 0), iota((ny, ny), 1)
    pos = jnp.where(a < mid, (a & 3) - 4, ny + (a & 3))
    onto = jnp.where((b & 7) < 4, ny - 4 + (b & 7), (b & 7) - 4)
    group = (a & (mid - 1)) >> 2
    e_y = jnp.where(group == (b >> 3), taps(jnp.abs(onto - pos)), 0.0).astype(BF16)
    e_y = jnp.concatenate([e_y, e_y], axis=0)
    zero = jnp.zeros((HALO, nx, ny), F32)
    for buf in (buf_a, buf_b):
        buf[pl.ds(0, HALO)] = zero
        buf[pl.ds(HALO + nz, HALO)] = zero

    for side, absent in ((0, gx == 0), (1, gx == n_gx - 1)):

        @pl.when(absent)
        def _(side=side):
            for k in range(STEPS):
                rx[k, side] = jnp.zeros(rx.shape[2:], F32)

    for side, absent in ((0, gy == 0), (1, gy == n_gy - 1)):

        @pl.when(absent)
        def _(side=side):
            for k in range(STEPS):
                ry[k, side] = jnp.zeros(ry.shape[2:], F32)

    lane = iota((half, ny), 1)
    lanes = iota((nx, ny), 1)
    outer = (lanes < 4) | (lanes >= ny - 4)

    def pack(v, k, g, q):
        z = g * CHUNK + q
        sx[k, 0, z] = v[nx - HALO :]
        sx[k, 1, z] = v[:HALO]
        top, low = v[:half], v[half:]
        first = (lane >> 2) == q
        second = (lane >> 2) == q + mid // 4
        s = 4 * q
        right = sy[k, 0, g]
        right = jnp.where(first, pltpu.roll(top, s + 4, 1), right)
        right = jnp.where(second, pltpu.roll(low, s + mid + 4, 1), right)
        sy[k, 0, g] = right
        left = sy[k, 1, g]
        left = jnp.where(second, pltpu.roll(top, s + mid, 1), left)
        left = jnp.where(first, pltpu.roll(low, s, 1), left)
        sy[k, 1, g] = left

    def halo_copies(k, g):
        zs = pl.ds(g * CHUNK, CHUNK)
        out = []
        for side, step, send_ok, recv_ok in (
            (0, 1, gx < n_gx - 1, gx > 0),
            (1, -1, gx > 0, gx < n_gx - 1),
        ):
            i = (k * chunks + g) * 2 + side
            copy = pltpu.make_async_remote_copy(
                src_ref=sx.at[k, side, zs], dst_ref=rx.at[k, side, zs],
                send_sem=sxs.at[i], recv_sem=rxs.at[i],
                device_id=(lax.rem(gx + step + n_gx, n_gx), gy), device_id_type=MESH,
            )
            out.append((copy, send_ok, recv_ok))
        for side, step, send_ok, recv_ok in (
            (0, 1, gy < n_gy - 1, gy > 0),
            (1, -1, gy > 0, gy < n_gy - 1),
        ):
            i = (k * chunks + g) * 2 + side
            copy = pltpu.make_async_remote_copy(
                src_ref=sy.at[k, side, g], dst_ref=ry.at[k, side, g],
                send_sem=sys_.at[i], recv_sem=rys.at[i],
                device_id=(gx, lax.rem(gy + step + n_gy, n_gy)), device_id_type=MESH,
            )
            out.append((copy, send_ok, recv_ok))
        return out

    def send_halo(k, g):
        for copy, send_ok, _ in halo_copies(k, g):
            pl.when(send_ok)(copy.start)

    def wait_halo(k, g):
        for copy, _, recv_ok in halo_copies(k, g):
            pl.when(recv_ok)(copy.wait_recv)

    order = tuple(range(1, chunks)) + (0,)

    loads[0].wait()
    for g in order:

        def first_pack(q, carry, g=g):
            pack(buf_a[HALO + g * CHUNK + q], 0, g, q)
            return carry

        lax.fori_loop(0, CHUNK, first_pack, 0)
    pl.semaphore_wait(barrier, n - 1)
    for g in order:
        send_halo(0, g)

    loads[1].wait()
    recv_dev = owner.shape[1]
    slots = snd.shape[2]
    upper = (iota((BLOCK, BLOCK), 0) < iota((BLOCK, BLOCK), 1)).astype(F32).astype(BF16)
    count = jnp.zeros((n, 1), F32)
    message = jnp.zeros((n * 8, slots), F32)
    part = iota((8, BLOCK), 0)
    shift = ny.bit_length() - 1
    for blk in range(recv_dev // BLOCK):
        rows = pl.ds(blk * BLOCK, BLOCK)
        enc = signs[0].astype(F32) * residual[0, rows, :]
        for s in range(1, residual.shape[0]):
            enc = enc + signs[s].astype(F32) * residual[s, rows, :]
        amps = lanes_dot(table[...], enc, precision=lax.Precision.HIGHEST)
        hi = amps.astype(BF16).astype(F32)
        c = cell[:, rows]
        at_x = (c >> shift).astype(F32)
        at_y = (c & (ny - 1)).astype(F32)
        payload = jnp.where((part & 1) == 0, hi, amps - hi)
        payload = jnp.where(part == 6, at_x, payload)
        payload = jnp.where(part == 7, at_y, payload)
        onehot = jnp.where(iota((n, BLOCK), 0) == owner[:, rows], 1.0, 0.0)
        before = jnp.dot(onehot.astype(BF16), upper, preferred_element_type=F32) + count
        count = count + jnp.sum(onehot, axis=1, keepdims=True)
        rank = jnp.sum(before * onehot, axis=0, keepdims=True)
        spread = (onehot[:, None, :] * payload[None]).reshape(n * 8, BLOCK).astype(BF16)
        slot = jnp.where(iota((slots, BLOCK), 0).astype(F32) == rank, 1.0, 0.0).astype(BF16)
        message = message + lanes_dot(spread, slot)
    snd[...] = message.reshape(n, 8, slots)
    got[me] = snd[me]

    def message_to(o):
        d = lax.rem(me + o, n)
        return pltpu.make_async_remote_copy(
            src_ref=snd.at[d], dst_ref=got.at[me], send_sem=snds.at[o], recv_sem=gots.at[o],
            device_id=(d // n_gy, lax.rem(d, n_gy)), device_id_type=MESH,
        )

    def post(o, carry):
        message_to(o).start()
        return carry

    lax.fori_loop(1, n, post, 0)

    def step_chunk(k, g, cur, prev):
        wait_halo(k, g)
        left, right = ry[k, 0, g], ry[k, 1, g]
        near = lane < mid
        edges = jnp.concatenate(
            [jnp.where(near, left, right), pltpu.roll(jnp.where(near, right, left), mid, 1)], axis=0
        )
        edge[...] = jnp.dot(split(edges, 1), e_y, preferred_element_type=F32)

        def body(j, carry):
            qs = [GROUP * j + i for i in range(GROUP)]
            vs = [cur[g * CHUNK + q + HALO] for q in qs]
            parts = []
            for v in vs:
                hi = v.astype(BF16)
                parts.append((hi, (v - hi.astype(F32)).astype(BF16)))
            along_y = jnp.dot(
                jnp.concatenate([jnp.concatenate(p, axis=1) for p in parts], axis=0), t_y,
                preferred_element_type=F32,
            )
            along_x = jnp.dot(
                t_x, jnp.concatenate([jnp.concatenate(p, axis=0) for p in parts], axis=1),
                preferred_element_type=F32,
            )
            overs = []
            for q in qs:
                z = g * CHUNK + q
                over = jnp.concatenate([rx[k, 0, z], rx[k, 1, z]], axis=0)
                over_hi = over.astype(BF16).astype(F32)
                overs.append(jnp.concatenate([over_hi, over - over_hi], axis=0).astype(BF16))
            border = jnp.dot(h_x, jnp.concatenate(overs, axis=1), preferred_element_type=F32)
            for i, (q, v) in enumerate(zip(qs, vs)):
                z = g * CHUNK + q
                cols = slice(i * ny, (i + 1) * ny)
                depth = TAPS[0] * (cur[z + HALO + 1] + cur[z + HALO - 1])
                for r in range(2, HALO + 1):
                    depth = depth + TAPS[r - 1] * (cur[z + HALO + r] + cur[z + HALO - r])
                lap = along_y[i * nx : (i + 1) * nx] + along_x[:, cols] + depth
                lap = lap + jnp.where(outer, pltpu.roll(edge[...], (2 * ny - 4 - 8 * q) & (ny - 1), 1), 0.0)
                lap = jnp.concatenate(
                    [lap[:8] + border[:8, cols], lap[8 : nx - 8], lap[nx - 8 :] + border[8:, cols]],
                    axis=0,
                )
                if k == 0:
                    speed = courant[z] * (1.0 / SCALE)
                    courant[z] = speed
                else:
                    speed = courant[z]
                nxt = (2.0 * v - prev[z + HALO]) + speed * lap
                prev[z + HALO] = nxt
                shot = snaps[k, z].astype(F32) * nxt
                image[z] = shot if k == 0 else image[z] + shot
                if k < STEPS - 1:
                    pack(nxt, k + 1, g, q)
            return carry

        lax.fori_loop(0, CHUNK // GROUP, body, 0)
        if k < STEPS - 1:
            send_halo(k + 1, g)

    def scatter():
        def arrive(o, carry):
            d = lax.rem(me - o + n, n)
            pltpu.make_async_remote_copy(
                src_ref=snd.at[d], dst_ref=got.at[d], send_sem=snds.at[o], recv_sem=gots.at[o],
                device_id=(d // n_gy, lax.rem(d, n_gy)), device_id_type=MESH,
            ).wait_recv()
            return carry

        lax.fori_loop(1, n, arrive, 0)
        planes[...] = jnp.zeros(planes.shape, F32)
        row_x = iota((nx, slots), 0).astype(F32)
        row_y = iota((ny, slots), 0).astype(F32)

        def gather(j, carry):
            lhs = [[] for _ in range(STEPS)]
            rhs = []
            for i in range(4):
                block = got[4 * j + i]
                at_x = row_x == block[6:7]
                at_y = jnp.where(row_y == block[7:8], 1.0, 0.0).astype(BF16)
                for k in range(STEPS):
                    for h in range(2):
                        lhs[k].append(
                            jnp.where(at_x, block[2 * k + h : 2 * k + h + 1], 0.0).astype(BF16)
                        )
                rhs += [at_y, at_y]
            lhs = jnp.concatenate([jnp.concatenate(l, axis=1) for l in lhs], axis=0)
            planes[...] += lanes_dot(lhs, jnp.concatenate(rhs, axis=1))
            return carry

        lax.fori_loop(0, n // 4, gather, 0)

    outs = []
    for load in loads[2:]:
        load.wait()
    for k in range(STEPS):
        cur, prev = (buf_a, buf_b) if k % 2 == 0 else (buf_b, buf_a)
        for g in order:
            if g == RECV_DEPTH // CHUNK:
                if k == 0:
                    scatter()
                at = HALO + RECV_DEPTH
                speed = courant[RECV_DEPTH] * (1.0 if k == 0 else SCALE)
                prev[at] = prev[at] - speed * planes[pl.ds(k * nx, nx), :]
            step_chunk(k, g, cur, prev)
            if k == STEPS - 1:
                zs = pl.ds(g * CHUNK, CHUNK)
                outs += [
                    pltpu.make_async_copy(
                        prev.at[pl.ds(HALO + g * CHUNK, CHUNK)], field_out.at[zs], out_sem.at[2 * g]
                    ),
                    pltpu.make_async_copy(image.at[zs], image_out.at[zs], out_sem.at[2 * g + 1]),
                ]
                outs[-2].start()
                outs[-1].start()

    def finish(o, carry):
        message_to(o).wait_send()
        return carry

    lax.fori_loop(1, n, finish, 0)
    for k in range(STEPS):
        for g in order:
            for copy, send_ok, _ in halo_copies(k, g):
                pl.when(send_ok)(copy.wait_send)
    for out in outs:
        out.wait()


def step_table(samples, steps):
    rows = np.arange(samples, dtype=np.float64)[None, :]
    cols = np.repeat(np.arange(steps, dtype=np.float64), 2)[:, None]
    table = np.cos(math.pi * (cols + 0.5) * (rows + 0.5) / samples) * math.sqrt(2.0 / samples)
    return np.concatenate([table, np.zeros((8 - 2 * steps, samples))]).astype(np.float32)


def shards(n_gx, n_gy, p_prev, p_cur, courant, snapshots, residual, rec_owner, rec_cell, signs):
    nz, nx, ny = p_cur.shape
    n = n_gx * n_gy
    recv_dev = rec_cell.shape[0]
    slots = -(-(2 * recv_dev // n) // 128) * 128
    chunks = nz // CHUNK
    anywhere = pl.BlockSpec(memory_space=pl.ANY)
    vmem = pl.BlockSpec(memory_space=pltpu.VMEM)
    dma = pltpu.SemaphoreType.DMA
    whole = jax.ShapeDtypeStruct(p_cur.shape, F32)
    return pl.pallas_call(
        functools.partial(kernel, n_gx, n_gy),
        out_shape=(whole, whole),
        in_specs=[pl.BlockSpec(memory_space=pltpu.SMEM)] + [vmem] * 3 + [anywhere] * 5,
        out_specs=(anywhere, anywhere),
        scratch_shapes=[
            pltpu.VMEM((nz + 2 * HALO, nx, ny), F32),
            pltpu.VMEM((nz + 2 * HALO, nx, ny), F32),
            pltpu.VMEM((nz, nx, ny), F32),
            pltpu.VMEM((STEPS, nz, nx, ny), BF16),
            pltpu.VMEM(residual.shape, F32),
            pltpu.VMEM((nz, nx, ny), F32),
            pltpu.VMEM((STEPS, 2, nz, HALO, ny), F32),
            pltpu.VMEM((STEPS, 2, nz, HALO, ny), F32),
            pltpu.VMEM((STEPS, 2, chunks, nx // 2, ny), F32),
            pltpu.VMEM((STEPS, 2, chunks, nx // 2, ny), F32),
            pltpu.VMEM((nx, ny), F32),
            pltpu.VMEM((STEPS * nx, ny), F32),
            pltpu.VMEM((n, 8, slots), F32),
            pltpu.VMEM((n, 8, slots), F32),
            dma((4 + STEPS,)),
            dma((2 * chunks,)),
            dma((2 * STEPS * chunks,)),
            dma((2 * STEPS * chunks,)),
            dma((2 * STEPS * chunks,)),
            dma((2 * STEPS * chunks,)),
            dma((n,)),
            dma((n,)),
        ],
        compiler_params=pltpu.CompilerParams(
            collective_id=0, has_side_effects=True, vmem_limit_bytes=60 * 1024 * 1024
        ),
        name="adjoint_steps",
    )(
        signs,
        rec_owner.reshape(1, recv_dev),
        rec_cell.reshape(1, recv_dev),
        jnp.asarray(step_table(NT, STEPS)),
        p_prev, p_cur, courant, snapshots, residual,
    )


def solution(mesh):
    placed = (
        P(None, "gx", "gy"),
        P(None, "gx", "gy"),
        P(None, "gx", "gy"),
        P(None, None, "gx", "gy"),
        P(None, ("gx", "gy"), None),
        P(("gx", "gy"), None),
        P(("gx", "gy")),
        P(),
    )
    return jax.shard_map(
        functools.partial(shards, mesh.shape["gx"], mesh.shape["gy"]),
        mesh=mesh,
        in_specs=placed,
        out_specs=(P(None, "gx", "gy"), P(None, "gx", "gy")),
        check_vma=False,
    )
```
